32 devices in a mesh: row: 8 (over z, x), col: 4 (over y, core).
Axes of the slice: x: 2, y: 2, z: 4, core: 2. Of those that a mesh axis runs over, the one named last changes fastest.
Arguments:
- x_vectors: bfloat16 [64, 32768], P(None, ('row', 'col')), may hold values from -6 to 6
- w_vectors: bfloat16 [64, 32768], P(None, ('row', 'col')), may hold values from -6 to 6
- order: int32 [32768], P(('row', 'col')), may hold values from 0 to 32767, as said below
- ubasis: bfloat16 [64, 32768], P(None, ('row', 'col')), may hold values from -0.75 to 0.75
- vbasis: bfloat16 [64, 32768], P(None, ('row', 'col')), may hold values from -0.75 to 0.75
- leaf_up_u: bfloat16 [64, 32768], P(None, ('row', 'col')), may hold values from -0.1875 to 0.1875
- leaf_up_v: bfloat16 [64, 32768], P(None, ('row', 'col')), may hold values from -0.1875 to 0.1875
- coupling: bfloat16 [64, 1048576], P(None, ('row', 'col')), may hold values from -0.1875 to 0.1875
- coupling_pairs: int32 [2, 16384], P(None, ('row', 'col')), may hold values from 0 to 511, as said below
- coupling_count: int32 [32], P(('row', 'col')), may hold values from 128 to 512, as said below
- near_blocks: bfloat16 [64, 524288], P(None, ('row', 'col')), may hold values from -0.1875 to 0.1875
- near_pairs: int32 [2, 8192], P(None, ('row', 'col')), may hold values from 0 to 511, as said below
- transfer_u: bfloat16 [64, 3840], replicated, may hold values from -0.5 to 0.5
- transfer_v: bfloat16 [64, 3840], replicated, may hold values from -0.5 to 0.5
- upper_coupling: bfloat16 [64, 3968], replicated, may hold values from -6 to 6
Outputs:
- y_product: bfloat16 [64, 32768], P(None, ('row', 'col'))
- z_product: bfloat16 [64, 32768], P(None, ('row', 'col'))
The draws below stay inside these ranges and needn't reach their ends.
Inputs may be any that keep to these rules, and one draw needn't show every extreme that they name: `order`: each block of 1024 consecutive entries is a permutation of that block's own positions. `coupling_pairs`: for slot b let d = b // 512, r = d // 4, c = d % 4. Entry [0, b] is a leaf of row group r, that is from r * 4 * 16 to (r + 1) * 4 * 16 - 1; entry [1, b] is a leaf l with (l // 16) % 4 == c. Slots of block d from coupling_count[d] onward are not used. `near_pairs`: for slot n let d = n // 256, r = d // 4, c = d % 4. Entry [0, n] is a leaf of row group r as for coupling_pairs; entry [1, n] is a leaf l with t = l // 16, t % 4 == c and t // 4 equal to r - 1, r or r + 1 modulo 8.
All inputs are finite; a program needn't handle non-finite values.
Results may differ from the reference program's by a relative error of at most 0.0063.
Values may be sent and summed in bfloat16 or wider, within the bound.
A program may use at most 192 MiB of HBM per device.

```python
import jax
import jax.numpy as jnp
from jax import lax

LEAF = 64
RANK = 64
NRHS = 64
LPD = 16
COUP_PER = 32
NEAR_PER = 16
ROW_DEVS = 8
COL_DEVS = 4
LEVELS = 5
PIECE = 1024
NLEAF = 512
N = 32768
CPD = 512
NPD = 256
NBLK = 16384
NNEAR = 8192
TNODES = 60
CNODES = 62


def shuffle_one(sub_key):
    return jax.random.permutation(sub_key, PIECE)


def draw_order(key, part):
    dev_count = ROW_DEVS * COL_DEVS
    keys = jax.random.split(key, dev_count)
    shuffled = jax.vmap(shuffle_one)(keys).astype(jnp.int32)
    offsets = jnp.arange(dev_count, dtype=jnp.int32)[:, None] * PIECE
    return (shuffled + offsets).reshape(-1).astype(jnp.int32)


def leaf_pairs(key, per_dev, near_only):
    dev_count = ROW_DEVS * COL_DEVS
    total = per_dev * dev_count
    first_key, second_key, third_key = jax.random.split(key, 3)
    owner = jnp.arange(total, dtype=jnp.int32) // per_dev
    row_group = owner // COL_DEVS
    col_group = owner % COL_DEVS
    row_leaf = row_group * COL_DEVS * LPD + jax.random.randint(first_key, (total,), 0, COL_DEVS * LPD, dtype=jnp.int32)
    if near_only:
        other_row = (row_group + jax.random.randint(second_key, (total,), -1, 2, dtype=jnp.int32)) % ROW_DEVS
    else:
        other_row = jax.random.randint(second_key, (total,), 0, ROW_DEVS, dtype=jnp.int32)
    inner = jax.random.randint(third_key, (total,), 0, LPD, dtype=jnp.int32)
    col_leaf = (other_row * COL_DEVS + col_group) * LPD + inner
    return jnp.stack([row_leaf, col_leaf]).astype(jnp.int32)


def draw_coupling_pairs(key, part):
    return leaf_pairs(jax.random.fold_in(key, 11), CPD, False)


def draw_near_pairs(key, part):
    return leaf_pairs(jax.random.fold_in(key, 23), NPD, True)


def draw_coupling_count(key, part):
    dev_count = ROW_DEVS * COL_DEVS
    first_key, second_key = jax.random.split(jax.random.fold_in(key, 37))
    shifts = jax.random.randint(first_key, (dev_count,), 0, 3, dtype=jnp.int32)
    forced = jax.random.randint(second_key, (), 0, dev_count, dtype=jnp.int32)
    shifts = jnp.where(jnp.arange(dev_count, dtype=jnp.int32) == forced, 0, shifts)
    return jnp.right_shift(jnp.full((dev_count,), CPD, jnp.int32), shifts).astype(jnp.int32)


def level_of(rng, extent, shards, least, high):
    gain = 1.0
    for position, shards_of in shards:
        draws = jax.random.uniform(jax.random.fold_in(jax.random.fold_in(rng, 6), position), (shards_of,), jnp.float32, least / len(shards), high / len(shards))
        gain = gain * jnp.repeat(jnp.exp(draws), extent[position] // shards_of).reshape((-1,) + (1,) * (len(extent) - 1 - position))
    return gain


def bell_draw(key, shape, deviation, most, cuts=(), kind=jnp.bfloat16):
    result = jax.random.normal(key, shape, jnp.float32) * deviation
    if len(cuts) > 0:
        result = level_of(key, shape, cuts, -0.22, 0.18) * result
    return jnp.clip(result, min=-most, max=most).astype(kind)


def setup_inputs(seed: int = 0) -> dict:
    key_list = jax.random.split(jax.random.key(seed), 16)
    x_vectors = bell_draw(key_list[0], (NRHS, N), 1.0, 6.0, ((1, 32),))
    w_vectors = bell_draw(key_list[1], (NRHS, N), 1.0, 6.0, ((1, 32),))
    order = draw_order(jax.random.fold_in(key_list[15], 71), 0)
    ubasis = bell_draw(key_list[3], (RANK, N), LEAF ** -0.5, 0.75, ((1, 32),))
    vbasis = bell_draw(key_list[4], (RANK, N), LEAF ** -0.5, 0.75, ((1, 32),))
    leaf_up_u = bell_draw(key_list[5], (RANK, NLEAF * RANK), (RANK * LPD) ** -0.5, 0.1875, ((1, 32),))
    leaf_up_v = bell_draw(key_list[6], (RANK, NLEAF * RANK), (RANK * LPD) ** -0.5, 0.1875, ((1, 32),))
    coupling = bell_draw(key_list[7], (RANK, NBLK * RANK), (RANK * COUP_PER // 2) ** -0.5, 0.1875, ((1, 32),))
    coupling_pairs = draw_coupling_pairs(jax.random.fold_in(key_list[15], 71), 0)
    coupling_count = draw_coupling_count(jax.random.fold_in(key_list[15], 71), 0)
    near_blocks = bell_draw(key_list[10], (LEAF, NNEAR * LEAF), (LEAF * NEAR_PER) ** -0.5, 0.1875, ((1, 32),))
    near_pairs = draw_near_pairs(jax.random.fold_in(key_list[15], 71), 0)
    transfer_u = bell_draw(key_list[12], (RANK, TNODES * RANK), (2 * RANK) ** -0.5, 0.5)
    transfer_v = bell_draw(key_list[13], (RANK, TNODES * RANK), (2 * RANK) ** -0.5, 0.5)
    upper_coupling = bell_draw(key_list[14], (RANK, CNODES * RANK), (LPD ** 0.5 * RANK ** -0.5), 6.0)
    return dict(x_vectors=x_vectors, w_vectors=w_vectors, order=order, ubasis=ubasis, vbasis=vbasis, leaf_up_u=leaf_up_u, leaf_up_v=leaf_up_v, coupling=coupling, coupling_pairs=coupling_pairs, coupling_count=coupling_count, near_blocks=near_blocks, near_pairs=near_pairs, transfer_u=transfer_u, transfer_v=transfer_v, upper_coupling=upper_coupling)


HIGHEST_PRECISION = lax.Precision.HIGHEST


def rounded(value):
    return lax.optimization_barrier(value.astype(jnp.bfloat16)).astype(jnp.float32)


def level_blocks(matrix_set, dev_count, level):
    node_count = dev_count >> level
    offset = 2 * dev_count - 2 * node_count
    columns = matrix_set[:, offset * RANK:(offset + node_count) * RANK]
    return columns.reshape(RANK, node_count, RANK).astype(jnp.float32)


def reference(x_vectors, w_vectors, order, ubasis, vbasis, leaf_up_u, leaf_up_v, coupling, coupling_pairs, coupling_count, near_blocks, near_pairs, transfer_u, transfer_v, upper_coupling):
    dev_count = ROW_DEVS * COL_DEVS
    leaf_total = dev_count * LPD
    x_perm = jnp.take(x_vectors, order, axis=1)
    w_perm = jnp.take(w_vectors, order, axis=1)
    x_leaves = x_perm.reshape(NRHS, leaf_total, LEAF).astype(jnp.float32)
    w_leaves = w_perm.reshape(NRHS, leaf_total, LEAF).astype(jnp.float32)
    v_leaves = vbasis.reshape(RANK, leaf_total, LEAF).astype(jnp.float32)
    u_leaves = ubasis.reshape(RANK, leaf_total, LEAF).astype(jnp.float32)
    x_coef = rounded(jnp.einsum("qlk,rlk->qlr", x_leaves, v_leaves))
    w_coef = rounded(jnp.einsum("qlk,rlk->qlr", w_leaves, u_leaves))
    up_v = leaf_up_v.reshape(RANK, dev_count, LPD, RANK).astype(jnp.float32)
    up_u = leaf_up_u.reshape(RANK, dev_count, LPD, RANK).astype(jnp.float32)
    x_node = rounded(jnp.einsum("qplr,rpls->pqs", x_coef.reshape(NRHS, dev_count, LPD, RANK), up_v))
    w_node = rounded(jnp.einsum("qplr,rpls->pqs", w_coef.reshape(NRHS, dev_count, LPD, RANK), up_u))

    y_terms = []
    z_terms = []
    for level in range(LEVELS):
        node_count = dev_count >> level
        sibling = jnp.arange(node_count, dtype=jnp.int32) ^ 1
        couple = level_blocks(upper_coupling, dev_count, level)
        y_terms.append(jnp.einsum("aqt,sat->aqs", x_node[sibling], couple))
        z_terms.append(jnp.einsum("aqs,sat->aqt", w_node[sibling], couple[:, sibling]))
        if level < LEVELS - 1:
            moved_x = jnp.einsum("aqr,ras->aqs", x_node, level_blocks(transfer_v, dev_count, level))
            moved_w = jnp.einsum("aqr,ras->aqs", w_node, level_blocks(transfer_u, dev_count, level))
            x_node = rounded(moved_x[0::2] + moved_x[1::2])
            w_node = rounded(moved_w[0::2] + moved_w[1::2])

    y_down = y_terms[LEVELS - 1]
    z_down = z_terms[LEVELS - 1]
    for level in range(LEVELS - 2, -1, -1):
        from_u = level_blocks(transfer_u, dev_count, level)
        from_v = level_blocks(transfer_v, dev_count, level)
        y_down = y_terms[level] + jnp.einsum("aqs,ras->aqr", jnp.repeat(y_down, 2, axis=0), from_u, precision=HIGHEST_PRECISION)
        z_down = z_terms[level] + jnp.einsum("aqs,ras->aqr", jnp.repeat(z_down, 2, axis=0), from_v, precision=HIGHEST_PRECISION)
    y_leafdown = jnp.einsum("pqs,rpls->qplr", y_down, up_u, precision=HIGHEST_PRECISION).reshape(NRHS, leaf_total, RANK)
    z_leafdown = jnp.einsum("pqs,rpls->qplr", z_down, up_v, precision=HIGHEST_PRECISION).reshape(NRHS, leaf_total, RANK)

    def add_couplings(device, sums):
        y_sum, z_sum = sums
        begin = (device * CPD).astype(jnp.int32)
        blocks = lax.dynamic_slice_in_dim(coupling, begin * RANK, CPD * RANK, 1)
        blocks = blocks.reshape(RANK, CPD, RANK).astype(jnp.float32)
        slot_pairs = lax.dynamic_slice_in_dim(coupling_pairs, begin, CPD, 1)
        live_mask = (jnp.arange(CPD, dtype=jnp.int32) < coupling_count[device]).astype(jnp.float32)[None, :, None]
        x_sel = jnp.take(x_coef, slot_pairs[1], axis=1)
        w_sel = jnp.take(w_coef, slot_pairs[0], axis=1)
        y_part = jnp.einsum("qbt,sbt->qbs", x_sel, blocks) * live_mask
        z_part = jnp.einsum("qbs,sbt->qbt", w_sel, blocks) * live_mask
        return y_sum.at[:, slot_pairs[0]].add(y_part), z_sum.at[:, slot_pairs[1]].add(z_part)

    zeros_coef = jnp.zeros((NRHS, leaf_total, RANK), jnp.float32)
    y_sum, z_sum = lax.fori_loop(0, dev_count, add_couplings, (zeros_coef, zeros_coef))

    def add_near(device, sums):
        y_raw, z_raw = sums
        begin = (device * NPD).astype(jnp.int32)
        blocks = lax.dynamic_slice_in_dim(near_blocks, begin * LEAF, NPD * LEAF, 1)
        blocks = blocks.reshape(LEAF, NPD, LEAF).astype(jnp.float32)
        slot_pairs = lax.dynamic_slice_in_dim(near_pairs, begin, NPD, 1)
        x_sel = jnp.take(x_leaves, slot_pairs[1], axis=1)
        w_sel = jnp.take(w_leaves, slot_pairs[0], axis=1)
        y_part = jnp.einsum("qnb,anb->qna", x_sel, blocks)
        z_part = jnp.einsum("qna,anb->qnb", w_sel, blocks)
        return y_raw.at[:, slot_pairs[0]].add(y_part), z_raw.at[:, slot_pairs[1]].add(z_part)

    zeros_raw = jnp.zeros((NRHS, leaf_total, LEAF), jnp.float32)
    y_raw, z_raw = lax.fori_loop(0, dev_count, add_near, (zeros_raw, zeros_raw))

    y_leaf = rounded(y_sum + y_leafdown)
    z_leaf = rounded(z_sum + z_leafdown)
    y_points = jnp.einsum("qlr,rlk->qlk", y_leaf, u_leaves) + y_raw
    z_points = jnp.einsum("qlr,rlk->qlk", z_leaf, v_leaves) + z_raw
    y_perm = y_points.reshape(NRHS, N).astype(jnp.bfloat16)
    z_perm = z_points.reshape(NRHS, N).astype(jnp.bfloat16)
    y_out = jnp.zeros((NRHS, N), jnp.bfloat16).at[:, order].set(y_perm)
    z_out = jnp.zeros((NRHS, N), jnp.bfloat16).at[:, order].set(z_perm)
    return (y_out, z_out)
```

```python
import functools

import jax
import jax.numpy as jnp
from jax import lax
from jax.experimental import pallas as pl
from jax.experimental.pallas import tpu as pltpu
from jax.sharding import PartitionSpec as P

BF = jnp.bfloat16
F32 = jnp.float32
VMEM = pl.BlockSpec(memory_space=pltpu.VMEM)
SMEM = pl.BlockSpec(memory_space=pltpu.SMEM)
NN = (((1,), (0,)), ((), ()))
NT = (((1,), (1,)), ((), ()))
VLIMIT = 60 * 1024 * 1024


def mm(a, b, dims=NN):
    return lax.dot_general(a, b, dims, preferred_element_type=F32)


def left_mask(half, dtype):
    lane = lax.broadcasted_iota(jnp.int32, (1, 2 * half), 1)
    return (lane < half).astype(F32).astype(dtype), (lane >= half).astype(F32).astype(dtype)


def diag2(v, ml, mr):
    return jnp.concatenate([v * ml, v * mr], axis=0)


def split2(v):
    hi = v.astype(BF)
    return hi, (v - hi.astype(F32)).astype(BF)


def mm2(v, b, dims):
    hi, lo = split2(v)
    return mm(hi, b, dims) + mm(lo, b, dims)


def one_hot(order_ref, base):
    n = order_ref.shape[1]
    src = lax.broadcasted_iota(jnp.int32, (n, n), 0)
    return jnp.where(src == order_ref[...] - base, 1.0, 0.0).astype(BF)


def up_kernel(base_ref, x_ref, w_ref, order_ref, v_ref, u_ref, ev_ref, eu_ref, xo_ref, wo_ref, xn_ref, wn_ref):
    q, n = x_ref.shape
    packs = xo_ref.shape[1]
    wide = xo_ref.shape[3]
    half = wide // 2
    ml, mr = left_mask(half, BF)
    hot = one_hot(order_ref, base_ref[0])
    both = mm(jnp.concatenate([x_ref[...], w_ref[...]], axis=0), hot).astype(BF)
    for side, (b_ref, e_ref, o_ref, n_ref) in enumerate(
        ((v_ref, ev_ref, xo_ref, xn_ref), (u_ref, eu_ref, wo_ref, wn_ref))
    ):
        pts = both[side * q:(side + 1) * q]
        node = jnp.zeros((q, wide), F32)
        for m in range(packs):
            cols = slice(m * wide, (m + 1) * wide)
            pm = pts[:, cols]
            cm = mm(pm, diag2(b_ref[:, cols], ml, mr), NT).astype(BF)
            o_ref[0, m] = cm
            o_ref[1, m] = pm
            node = node + mm(cm, diag2(e_ref[:, cols], ml, mr))
        n_ref[...] = (node + pltpu.roll(node, half, 1)).astype(BF)[:, :half]


def slot_kernel(ids_ref, x_ref, w_ref, s_ref, d_ref, y_ref, z_ref, xc, xp, wc, wp, yc, yn, zc, zn):
    rows, _, packs, q, wide = x_ref.shape
    cols = w_ref.shape[0]
    half = wide // 2
    ml, mr = left_mask(half, BF)
    slots = s_ref.shape[1] // half
    nears = d_ref.shape[1] // half
    o_row, o_col, n_row, n_col = 0, slots, 2 * slots, 2 * slots + nears
    live = ids_ref[2 * slots + 2 * nears]
    my_row = ids_ref[2 * slots + 2 * nears + 1]
    isl = lax.broadcasted_iota(jnp.int32, (q, wide), 1) < half
    lane = lax.broadcasted_iota(jnp.int32, (1, wide), 1)
    for acc in (yc, yn, zc, zn):
        def clear(i, carry, acc=acc):
            acc[i] = jnp.zeros(acc.shape[1:], F32)
            return carry
        lax.fori_loop(0, acc.shape[0], clear, 0)

    def widen(src, table, at):
        v = src[...].astype(F32)
        r = pltpu.roll(v, half, 1)
        table[at] = jnp.where(isl, v, r).astype(BF)
        table[at + 1] = jnp.where(isl, r, v).astype(BF)

    def fill_x(i, carry):
        for m in range(packs):
            widen(x_ref.at[i, 0, m], xc, 2 * (i * packs + m))
        return carry

    def fill_w(i, carry):
        for m in range(packs):
            widen(w_ref.at[i, 0, m], wc, 2 * (i * packs + m))
            widen(w_ref.at[i, 1, m], wp, 2 * (i * packs + m))
        return carry

    lax.fori_loop(0, rows, fill_x, 0)
    lax.fori_loop(0, cols, fill_w, 0)
    for k in range(3):
        src = lax.rem(my_row + (k + rows - 1), rows)
        for m in range(packs):
            widen(x_ref.at[src, 1, m], xp, 2 * (k * packs + m))

    def run(mat, xt, wt, ya, za, row_at, col_at, masked, steps, unroll):
        def step(g, carry):
            work = []
            for k in range(unroll):
                p = g * unroll + k
                i0, i1 = ids_ref[row_at + 2 * p], ids_ref[row_at + 2 * p + 1]
                j0, j1 = ids_ref[col_at + 2 * p], ids_ref[col_at + 2 * p + 1]
                blk = mat[:, pl.ds(pl.multiple_of(p * wide, wide), wide)]
                if masked:
                    left_ok = jnp.where(2 * p < live, 1.0, 0.0)
                    right_ok = jnp.where(2 * p + 1 < live, 1.0, 0.0)
                    a = jnp.where(lane < half, left_ok, 0.0).astype(BF)
                    b = jnp.where(lane < half, 0.0, right_ok).astype(BF)
                else:
                    a, b = ml, mr
                pair = jnp.concatenate([blk * a, blk * b], axis=0)
                xs = xt[j0] * ml + xt[j1] * mr
                ws = wt[i0] * ml + wt[i1] * mr
                work.append((i0, i1, j0, j1, mm(xs, pair, NT), mm(ws, pair)))
            for i0, i1, j0, j1, yv, zv in work:
                ya[i0] += jnp.where(isl, yv, 0.0)
                ya[i1] += jnp.where(isl, 0.0, yv)
                za[j0] += jnp.where(isl, zv, 0.0)
                za[j1] += jnp.where(isl, 0.0, zv)
            return carry
        lax.fori_loop(0, steps, step, 0)

    unroll = 4
    run(s_ref, xc, wc, yc, zc, o_row, o_col, True, (live + 2 * unroll - 1) // (2 * unroll), unroll)
    run(d_ref, xp, wp, yn, zn, n_row, n_col, False, nears // (2 * unroll), unroll)

    def fold(acc, at):
        a, b = acc[at], acc[at + 1]
        return jnp.where(isl, a + pltpu.roll(a, half, 1), b + pltpu.roll(b, half, 1))

    def out_y(i, carry):
        for m in range(packs):
            y_ref[i, 0, m] = fold(yc, 2 * (i * packs + m)).astype(y_ref.dtype)
            y_ref[i, 1, m] = fold(yn, 2 * (i * packs + m)).astype(y_ref.dtype)
        return carry

    def out_z(i, carry):
        rel = lax.rem(i - my_row + (rows + 1), rows)
        for m in range(packs):
            z_ref[i, 0, m] = fold(zc, 2 * (i * packs + m)).astype(z_ref.dtype)

        @pl.when(rel < 3)
        def _():
            for m in range(packs):
                z_ref[i, 1, m] = fold(zn, 2 * (rel * packs + m)).astype(z_ref.dtype)

        @pl.when(rel >= 3)
        def _():
            for m in range(packs):
                z_ref[i, 1, m] = jnp.zeros((q, wide), z_ref.dtype)
        return carry

    lax.fori_loop(0, cols, out_y, 0)
    lax.fori_loop(0, rows, out_z, 0)


def down_kernel(base_ref, y_ref, z_ref, yd_ref, zd_ref, order_ref, u_ref, v_ref, eu_ref, ev_ref, yo_ref, zo_ref):
    _, packs, q, wide = y_ref.shape
    half = wide // 2
    ml, mr = left_mask(half, BF)
    hot = one_hot(order_ref, base_ref[0])
    perms = []
    for s_ref, d_ref, b_ref, e_ref in ((y_ref, yd_ref, u_ref, eu_ref), (z_ref, zd_ref, v_ref, ev_ref)):
        down = jnp.concatenate([d_ref[...], d_ref[...]], axis=1)
        parts = []
        for m in range(packs):
            cs = slice(m * wide, (m + 1) * wide)
            leaf = (s_ref[0, m] + mm2(down, diag2(e_ref[:, cs], ml, mr), NT)).astype(BF)
            parts.append((mm(leaf, diag2(b_ref[:, cs], ml, mr)) + s_ref[1, m]).astype(BF))
        perms.append(jnp.concatenate(parts, axis=1))
    out = mm(jnp.concatenate(perms, axis=0), hot, NT).astype(BF)
    yo_ref[...] = out[:q]
    zo_ref[...] = out[q:]


def from_partner(block, axis, bit):
    count = lax.axis_size(axis)
    route = []
    for low in range(count):
        high = low | 1 << bit
        if high != low and high < count:
            route += [(low, high), (high, low)]
    return lax.ppermute(block, axis, route)


def node_block(matrix_set, node_id, node_width):
    return lax.dynamic_slice_in_dim(matrix_set, node_id * node_width, node_width, 1)


def tree(x_level, w_level, transfer_u, transfer_v, upper_coupling, rank):
    dev_count = lax.axis_size(("row", "col"))
    levels = dev_count.bit_length() - 1
    me = lax.axis_index(("row", "col"))
    y_terms, z_terms = [], []
    for level in range(levels):
        pair = jnp.concatenate([x_level, w_level], axis=1)
        sib = from_partner(pair, ("row", "col"), level)
        sib_x, sib_w = sib[:, :rank], sib[:, rank:]
        off = 2 * dev_count - 2 * (dev_count >> level)
        own = me >> level
        other = own ^ 1
        y_terms.append(mm(sib_x, node_block(upper_coupling, off + own, rank), NT))
        z_terms.append(mm(sib_w, node_block(upper_coupling, off + other, rank)))
        if level < levels - 1:
            x_level, w_level = (
                (mm(a, node_block(t, off + own, rank)) + mm(b, node_block(t, off + other, rank))).astype(BF)
                for a, b, t in ((x_level, sib_x, transfer_v), (w_level, sib_w, transfer_u))
            )
    y_down, z_down = y_terms[-1], z_terms[-1]
    for level in range(levels - 2, -1, -1):
        off = 2 * dev_count - 2 * (dev_count >> level)
        own = me >> level
        y_down = y_terms[level] + mm2(y_down, node_block(transfer_u, off + own, rank), NT)
        z_down = z_terms[level] + mm2(z_down, node_block(transfer_v, off + own, rank), NT)
    return y_down, z_down


def per_device(
    x_vectors,
    w_vectors,
    order,
    ubasis,
    vbasis,
    leaf_up_u,
    leaf_up_v,
    coupling,
    coupling_pairs,
    coupling_count,
    near_blocks,
    near_pairs,
    transfer_u,
    transfer_v,
    upper_coupling,
):
    q, piece = x_vectors.shape
    rank = ubasis.shape[0]
    leaves = leaf_up_u.shape[1] // rank
    packs = leaves // 2
    wide = 2 * rank
    slots = coupling_pairs.shape[1]
    nears = near_pairs.shape[1]
    rows = lax.axis_size("row")
    cols = lax.axis_size("col")
    me = lax.axis_index(("row", "col"))
    my_row = lax.axis_index("row")
    base = (me * piece).astype(jnp.int32).reshape(1)
    row_base = my_row * cols * leaves
    order2 = order.reshape(1, piece)
    params = pltpu.CompilerParams(vmem_limit_bytes=VLIMIT)
    x_out, w_out, x_node, w_node = pl.pallas_call(
        up_kernel,
        out_shape=(
            jax.ShapeDtypeStruct((2, packs, q, wide), BF),
            jax.ShapeDtypeStruct((2, packs, q, wide), BF),
            jax.ShapeDtypeStruct((q, rank), BF),
            jax.ShapeDtypeStruct((q, rank), BF),
        ),
        in_specs=[SMEM] + [VMEM] * 7,
        out_specs=(VMEM,) * 4,
        compiler_params=params,
    )(base, x_vectors, w_vectors, order2, vbasis, ubasis, leaf_up_v, leaf_up_u)
    x_all = lax.all_gather(x_out, "row", axis=0)
    w_all = lax.all_gather(w_out, "col", axis=0)
    tiles = near_pairs[1] // leaves // cols
    ids = jnp.concatenate(
        [
            coupling_pairs[0] - row_base,
            coupling_pairs[1] // leaves // cols * leaves + coupling_pairs[1] % leaves,
            near_pairs[0] - row_base,
            (tiles - my_row + rows + 1) % rows * leaves + near_pairs[1] % leaves,
            coupling_count,
            my_row.reshape(1).astype(jnp.int32),
        ]
    )
    y_part, z_part = pl.pallas_call(
        slot_kernel,
        out_shape=(
            jax.ShapeDtypeStruct((cols, 2, packs, q, wide), F32),
            jax.ShapeDtypeStruct((rows, 2, packs, q, wide), F32),
        ),
        in_specs=[SMEM] + [VMEM] * 4,
        out_specs=(VMEM,) * 2,
        scratch_shapes=[
            pltpu.VMEM((rows * leaves, q, wide), BF),
            pltpu.VMEM((3 * leaves, q, wide), BF),
            pltpu.VMEM((cols * leaves, q, wide), BF),
            pltpu.VMEM((cols * leaves, q, wide), BF),
            pltpu.VMEM((cols * leaves, q, wide), F32),
            pltpu.VMEM((cols * leaves, q, wide), F32),
            pltpu.VMEM((rows * leaves, q, wide), F32),
            pltpu.VMEM((3 * leaves, q, wide), F32),
        ],
        compiler_params=params,
    )(ids, x_all, w_all, coupling, near_blocks)
    y_down, z_down = tree(x_node, w_node, transfer_u, transfer_v, upper_coupling, rank)
    y_own = lax.psum_scatter(y_part, "col", scatter_dimension=0, tiled=False)
    z_own = lax.psum_scatter(z_part, "row", scatter_dimension=0, tiled=False)
    return pl.pallas_call(
        down_kernel,
        out_shape=(jax.ShapeDtypeStruct((q, piece), BF),) * 2,
        in_specs=[SMEM] + [VMEM] * 9,
        out_specs=(VMEM,) * 2,
        compiler_params=params,
    )(base, y_own, z_own, y_down, z_down, order2, ubasis, vbasis, leaf_up_u, leaf_up_v)


def solution(mesh):
    both = P(None, ("row", "col"))
    flat = P(("row", "col"))
    return jax.shard_map(
        per_device,
        mesh=mesh,
        in_specs=(both, both, flat, both, both, both, both, both, both, flat, both, both, P(), P(), P()),
        out_specs=(both, both),
        check_vma=False,
    )
```

```python
import functools

import jax
import jax.numpy as jnp
from jax import lax
from jax.experimental import pallas as pl
from jax.experimental.pallas import tpu as pltpu
from jax.sharding import PartitionSpec as P

BF = jnp.bfloat16
F32 = jnp.float32
VMEM = pl.BlockSpec(memory_space=pltpu.VMEM)
SMEM = pl.BlockSpec(memory_space=pltpu.SMEM)
NN = (((1,), (0,)), ((), ()))
NT = (((1,), (1,)), ((), ()))
VLIMIT = 60 * 1024 * 1024


def mm(a, b, dims=NN):
    return lax.dot_general(a, b, dims, preferred_element_type=F32)


def left_mask(half, dtype):
    lane = lax.broadcasted_iota(jnp.int32, (1, 2 * half), 1)
    return (lane < half).astype(F32).astype(dtype), (lane >= half).astype(F32).astype(dtype)


def diag2(v, ml, mr):
    return jnp.concatenate([v * ml, v * mr], axis=0)


def split2(v):
    hi = v.astype(BF)
    return hi, (v - hi.astype(F32)).astype(BF)


def mm2(v, b, dims):
    hi, lo = split2(v)
    return mm(hi, b, dims) + mm(lo, b, dims)


def one_hot(order_ref, base):
    n = order_ref.shape[1]
    src = lax.broadcasted_iota(jnp.int32, (n, n), 0)
    return jnp.where(src == order_ref[...] - base, 1.0, 0.0).astype(BF)


def grid_of(rows):
    inner = 1 << ((rows.bit_length() - 1) // 2)
    return rows // inner, inner


def greet(rows, cols, r, c):
    bar = pltpu.get_barrier_semaphore()
    for d in range(1, rows):
        pl.semaphore_signal(bar, inc=1, device_id={"row": lax.rem(r + d, rows)}, device_id_type=pl.DeviceIdType.MESH)
    for d in range(1, cols):
        pl.semaphore_signal(bar, inc=1, device_id={"col": lax.rem(c + d, cols)}, device_id_type=pl.DeviceIdType.MESH)
    return bar


def push(src, dst, sems, at, axis, peer):
    copy = pltpu.make_async_remote_copy(
        src_ref=src,
        dst_ref=dst,
        send_sem=sems.at[(0, *at)],
        recv_sem=sems.at[(1, *at)],
        device_id={axis: peer},
        device_id_type=pl.DeviceIdType.MESH,
    )
    copy.start()
    return copy


def chunk_at(ref, at, wide):
    return ref[:, pl.ds(pl.multiple_of(at * wide, wide), wide)]


def combine(v0, v1, fv, fu, ml, mr, isl, half):
    xp = jnp.where(isl, v0, pltpu.roll(v1, half, 1)).astype(BF)
    wp = jnp.where(isl, pltpu.roll(v0, half, 1), v1).astype(BF)
    x = mm(xp, diag2(fv, ml, mr))
    w = mm(wp, diag2(fu, ml, mr))
    return jnp.where(isl, x + pltpu.roll(x, half, 1), w + pltpu.roll(w, half, 1)).astype(BF)


def up_kernel(rows, cols, x_ref, w_ref, order_ref, v_ref, u_ref, ev_ref, eu_ref, fu_ref, fv_ref,
              xc_ref, xp_ref, wa_ref, n0_ref, n2_ref, na_sem, nb_sem, z_sem, x_sem, p_sem, w_sem):
    q, n = x_ref.shape
    packs = xc_ref.shape[1]
    wide = xc_ref.shape[3]
    half = wide // 2
    deep, inner = grid_of(rows)
    r = lax.axis_index("row")
    c = lax.axis_index("col")
    zi = r // inner
    xi = lax.rem(r, inner)
    bar = greet(rows, cols, r, c)
    ml, mr = left_mask(half, BF)
    isl = lax.broadcasted_iota(jnp.int32, (q, wide), 1) < half
    hot = one_hot(order_ref, (r * cols + c) * n)
    both = mm(jnp.concatenate([x_ref[...], w_ref[...]], axis=0), hot).astype(BF)
    folds = []
    for side, (b_ref, e_ref) in enumerate(((v_ref, ev_ref), (u_ref, eu_ref))):
        pts = both[side * q:(side + 1) * q]
        node = jnp.zeros((q, wide), F32)
        for m in range(packs):
            cs = slice(m * wide, (m + 1) * wide)
            pm = pts[:, cs]
            cm = mm(pm, diag2(b_ref[:, cs], ml, mr), NT).astype(BF)
            if side == 0:
                xc_ref[r, m] = cm
                xp_ref[1, m] = pm
            else:
                wa_ref[c, 0, m] = cm
                wa_ref[c, 1, m] = pm
            node = node + mm(cm, diag2(e_ref[:, cs], ml, mr))
        folds.append(node + pltpu.roll(node, half, 1))
    n0_ref[c] = jnp.where(isl, folds[0], folds[1]).astype(BF)
    pl.semaphore_wait(bar, rows + cols - 2)
    node_a = [
        push(n0_ref.at[c], n0_ref.at[c], na_sem, (d - 1,), "col", lax.rem(c + d, cols)) for d in range(1, cols)
    ]
    own = xc_ref.at[r]
    along = [
        push(own, own, z_sem, (d - 1,), "row", lax.rem(zi + d, deep) * inner + xi) for d in range(1, deep)
    ]
    across = [
        push(own, own, x_sem, (0, d - 1), "row", zi * inner + lax.rem(xi + d, inner)) for d in range(1, inner)
    ]
    points = [
        push(xp_ref.at[1], xp_ref.at[0], p_sem, (0,), "row", lax.rem(r + 1, rows)),
        push(xp_ref.at[1], xp_ref.at[2], p_sem, (1,), "row", lax.rem(r + rows - 1, rows)),
    ]
    wide_w = [
        push(wa_ref.at[c], wa_ref.at[c], w_sem, (d - 1,), "col", lax.rem(c + d, cols)) for d in range(1, cols)
    ]
    for copy in node_a:
        copy.wait_recv()
    dev_count = rows * cols
    vals = [n0_ref[i].astype(F32) for i in range(cols)]
    level = 0
    while len(vals) > 1:
        off = dev_count - (dev_count >> level)
        count = len(vals) // 2
        nxt = []
        for i in range(count):
            at = off + r * count + i
            nxt.append(
                combine(vals[2 * i], vals[2 * i + 1], chunk_at(fv_ref, at, wide), chunk_at(fu_ref, at, wide), ml, mr, isl, half)
            )
        vals = [v.astype(F32) for v in nxt]
        level += 1
    n2_ref[r] = vals[0].astype(BF)
    node_b = [
        push(n2_ref.at[r], n2_ref.at[r], nb_sem, (d - 1,), "row", lax.rem(r + d, rows)) for d in range(1, rows)
    ]
    for d in range(1, deep):
        along[d - 1].wait_recv()
        got = xc_ref.at[lax.rem(zi + deep - d, deep) * inner + xi]
        across += [
            push(got, got, x_sem, (d, e - 1), "row", zi * inner + lax.rem(xi + e, inner)) for e in range(1, inner)
        ]
    for copy in node_b + across + points + wide_w:
        copy.wait_recv()
    for copy in node_a + node_b + along + across + points + wide_w:
        copy.wait_send()


def slot_kernel(ids_ref, x_ref, p_ref, w_ref, s_ref, d_ref, y_ref, z_ref, n_ref, xc, xp, wc, wp, yc, yn, zc, zn):
    rows, packs, q, wide = x_ref.shape
    cols = w_ref.shape[0]
    half = wide // 2
    ml, mr = left_mask(half, BF)
    slots = s_ref.shape[1] // half
    nears = d_ref.shape[1] // half
    o_row, o_col, n_row, n_col = 0, slots, 2 * slots, 2 * slots + nears
    live = ids_ref[2 * slots + 2 * nears]
    isl = lax.broadcasted_iota(jnp.int32, (q, wide), 1) < half
    lane = lax.broadcasted_iota(jnp.int32, (1, wide), 1)
    for acc in (yc, yn, zc, zn):
        def clear(i, carry, acc=acc):
            acc[i] = jnp.zeros(acc.shape[1:], F32)
            return carry
        lax.fori_loop(0, acc.shape[0], clear, 0)

    def widen(src, table, at):
        v = src[...].astype(F32)
        r = pltpu.roll(v, half, 1)
        table[at] = jnp.where(isl, v, r).astype(BF)
        table[at + 1] = jnp.where(isl, r, v).astype(BF)

    def fill_x(i, carry):
        for m in range(packs):
            widen(x_ref.at[i, m], xc, 2 * (i * packs + m))
        return carry

    def fill_w(i, carry):
        for m in range(packs):
            widen(w_ref.at[i, 0, m], wc, 2 * (i * packs + m))
            widen(w_ref.at[i, 1, m], wp, 2 * (i * packs + m))
        return carry

    lax.fori_loop(0, rows, fill_x, 0)
    lax.fori_loop(0, cols, fill_w, 0)
    for k in range(3):
        for m in range(packs):
            widen(p_ref.at[k, m], xp, 2 * (k * packs + m))

    def run(mat, xt, wt, ya, za, row_at, col_at, masked, steps, unroll):
        def step(g, carry):
            work = []
            for k in range(unroll):
                p = g * unroll + k
                i0, i1 = ids_ref[row_at + 2 * p], ids_ref[row_at + 2 * p + 1]
                j0, j1 = ids_ref[col_at + 2 * p], ids_ref[col_at + 2 * p + 1]
                blk = mat[:, pl.ds(pl.multiple_of(p * wide, wide), wide)]
                if masked:
                    left_ok = jnp.where(2 * p < live, 1.0, 0.0)
                    right_ok = jnp.where(2 * p + 1 < live, 1.0, 0.0)
                    a = jnp.where(lane < half, left_ok, 0.0).astype(BF)
                    b = jnp.where(lane < half, 0.0, right_ok).astype(BF)
                else:
                    a, b = ml, mr
                pair = jnp.concatenate([blk * a, blk * b], axis=0)
                xs = xt[j0] * ml + xt[j1] * mr
                ws = wt[i0] * ml + wt[i1] * mr
                work.append((i0, i1, j0, j1, mm(xs, pair, NT), mm(ws, pair)))
            for i0, i1, j0, j1, yv, zv in work:
                ya[i0] += jnp.where(isl, yv, 0.0)
                ya[i1] += jnp.where(isl, 0.0, yv)
                za[j0] += jnp.where(isl, zv, 0.0)
                za[j1] += jnp.where(isl, 0.0, zv)
            return carry
        lax.fori_loop(0, steps, step, 0)

    unroll = 4
    run(s_ref, xc, wc, yc, zc, o_row, o_col, True, (live + 2 * unroll - 1) // (2 * unroll), unroll)
    run(d_ref, xp, wp, yn, zn, n_row, n_col, False, nears // (2 * unroll), unroll)

    def fold(acc, at):
        a, b = acc[at], acc[at + 1]
        return jnp.where(isl, a + pltpu.roll(a, half, 1), b + pltpu.roll(b, half, 1))

    def out_y(i, carry):
        for m in range(packs):
            y_ref[i, 0, m] = fold(yc, 2 * (i * packs + m)).astype(y_ref.dtype)
            y_ref[i, 1, m] = fold(yn, 2 * (i * packs + m)).astype(y_ref.dtype)
        return carry

    def out_z(i, carry):
        for m in range(packs):
            z_ref[i, m] = fold(zc, 2 * (i * packs + m)).astype(z_ref.dtype)
        return carry

    def out_n(i, carry):
        for m in range(packs):
            n_ref[i, m] = fold(zn, 2 * (i * packs + m)).astype(n_ref.dtype)
        return carry

    lax.fori_loop(0, cols, out_y, 0)
    lax.fori_loop(0, rows, out_z, 0)
    lax.fori_loop(0, 3, out_n, 0)


def down_kernel(rows, cols, y_ref, z_ref, n_ref, n0_ref, n2_ref, order_ref, u_ref, v_ref, eu_ref, ev_ref, fu_ref, fv_ref,
                s_ref, yo_ref, zo_ref, y_in, z1_in, z1_out, z2_in, zn_in, nodes, y_sem, z1_sem, z2_sem, n_sem):
    _, packs, q, wide = z_ref.shape
    half = wide // 2
    deep, inner = grid_of(rows)
    dev_count = rows * cols
    r = lax.axis_index("row")
    c = lax.axis_index("col")
    me = r * cols + c
    zi = r // inner
    xi = lax.rem(r, inner)
    bar = greet(rows, cols, r, c)
    ml, mr = left_mask(half, BF)
    isl = lax.broadcasted_iota(jnp.int32, (q, wide), 1) < half
    hot = one_hot(order_ref, me * order_ref.shape[1])
    pl.semaphore_wait(bar, rows + cols - 2)
    first = {}
    for d in list(range(1, deep)) + [0]:
        to = lax.rem(zi + d, deep) * inner
        first[d] = []
        for e in range(1, inner):
            peer = lax.rem(xi + e, inner)
            first[d].append(
                push(z_ref.at[to + peer], z1_in.at[d, e - 1], z1_sem, (d, e - 1), "row", zi * inner + peer)
            )
    near = [
        push(n_ref.at[0], zn_in.at[0], n_sem, (0,), "row", lax.rem(r + rows - 1, rows)),
        push(n_ref.at[2], zn_in.at[1], n_sem, (1,), "row", lax.rem(r + 1, rows)),
    ]
    y_copies = []
    for d in range(1, cols):
        peer = lax.rem(c + d, cols)
        y_copies.append(push(y_ref.at[peer], y_in.at[d - 1], y_sem, (d - 1,), "col", peer))

    second = []
    for d in range(1, deep):
        for copy in first[d]:
            copy.wait_recv()
        to = lax.rem(zi + d, deep) * inner + xi
        for m in range(packs):
            total = z_ref[to, m].astype(F32)
            for e in range(inner - 1):
                total = total + z1_in[d, e, m].astype(F32)
            z1_out[d - 1, m] = total.astype(BF)
        second.append(push(z1_out.at[d - 1], z2_in.at[d - 1], z2_sem, (d - 1,), "row", to))

    levels = dev_count.bit_length() - 1
    starts = []
    at = 0
    vals = None
    for level in range(levels):
        if level == 0:
            vals = [n0_ref[i].astype(F32) for i in range(cols)]
            split = r
        elif cols >> level == 1:
            vals = [n2_ref[i].astype(F32) for i in range(rows)]
            split = 0
        starts.append((at, c >> level if cols >> level > 1 else me >> level))
        for i, v in enumerate(vals):
            nodes[at + i] = v
        at += len(vals)
        off = dev_count - (dev_count >> level)
        count = len(vals) // 2
        if level < levels - 1 and count * 2 == len(vals) and not (cols >> level == 2):
            vals = [
                combine(
                    vals[2 * i],
                    vals[2 * i + 1],
                    chunk_at(fv_ref, off + split * count + i, wide),
                    chunk_at(fu_ref, off + split * count + i, wide),
                    ml, mr, isl, half,
                ).astype(F32)
                for i in range(count)
            ]

    lane_half = (lax.broadcasted_iota(jnp.int32, (q, wide), 1) >= half).astype(jnp.int32)

    def turned(v, chunk, side):
        return mm2(jnp.where(lane_half == side, v, 0.0), jnp.concatenate([chunk, chunk], axis=0), NT)

    y_down = z_down = None
    for level in range(levels - 1, -1, -1):
        start, local = starts[level]
        own = me >> level
        side = lax.rem(own, 2)
        sib = nodes[start + local + 1 - 2 * lax.rem(local, 2)]
        rolled = pltpu.roll(sib, half, 1)
        xs = jnp.where(isl, sib, rolled)
        ws = jnp.where(isl, rolled, 0.0).astype(BF)
        at = dev_count - (dev_count >> level) + own // 2
        cup = chunk_at(s_ref, at, wide)
        dup = jnp.concatenate([cup, cup], axis=0)
        y_term = mm(jnp.where(lane_half == side, xs, 0.0).astype(BF), dup, NT)
        z_raw = jnp.where(lane_half == 1 - side, mm(ws, dup), 0.0)
        z_term = z_raw + pltpu.roll(z_raw, half, 1)
        if level < levels - 1:
            y_term = y_term + turned(y_down, chunk_at(fu_ref, at, wide), side)
            z_term = z_term + turned(z_down, chunk_at(fv_ref, at, wide), side)
        y_down, z_down = y_term, z_term

    perms = []
    for flip, (down, b_ref, e_ref) in enumerate(((y_down, u_ref, eu_ref), (z_down, v_ref, ev_ref))):
        if flip == 0:
            for copy in y_copies:
                copy.wait_recv()
        else:
            for copy in first[0] + second + near:
                copy.wait_recv()
        parts = []
        for m in range(packs):
            cs = slice(m * wide, (m + 1) * wide)
            if flip == 0:
                coef, raw = y_ref[c, 0, m].astype(F32), y_ref[c, 1, m].astype(F32)
                for d in range(cols - 1):
                    coef = coef + y_in[d, 0, m].astype(F32)
                    raw = raw + y_in[d, 1, m].astype(F32)
            else:
                coef, raw = z_ref[r, m].astype(F32), n_ref[1, m].astype(F32)
                for e in range(inner - 1):
                    coef = coef + z1_in[0, e, m].astype(F32)
                for d in range(deep - 1):
                    coef = coef + z2_in[d, m].astype(F32)
                for k in range(2):
                    raw = raw + zn_in[k, m].astype(F32)
            leaf = (coef + mm2(down, diag2(e_ref[:, cs], ml, mr), NT)).astype(BF)
            parts.append((mm(leaf, diag2(b_ref[:, cs], ml, mr)) + raw).astype(BF))
        perms.append(jnp.concatenate(parts, axis=1))
    out = mm(jnp.concatenate(perms, axis=0), hot, NT).astype(BF)
    yo_ref[...] = out[:q]
    zo_ref[...] = out[q:]
    for copies in (*first.values(), second, near, y_copies):
        for copy in copies:
            copy.wait_send()


def per_device(
    x_vectors,
    w_vectors,
    order,
    ubasis,
    vbasis,
    leaf_up_u,
    leaf_up_v,
    coupling,
    coupling_pairs,
    coupling_count,
    near_blocks,
    near_pairs,
    transfer_u,
    transfer_v,
    upper_coupling,
):
    q, piece = x_vectors.shape
    rank = ubasis.shape[0]
    leaves = leaf_up_u.shape[1] // rank
    packs = leaves // 2
    wide = 2 * rank
    rows = lax.axis_size("row")
    cols = lax.axis_size("col")
    deep, inner = grid_of(rows)
    my_row = lax.axis_index("row")
    row_base = my_row * cols * leaves
    order2 = order.reshape(1, piece)

    def shape(*lead):
        return jax.ShapeDtypeStruct((*lead, q, wide), BF)

    def buf(*lead, dtype=BF):
        return pltpu.VMEM((*lead, q, wide), dtype)

    def sems(*lead):
        return pltpu.SemaphoreType.DMA((2, *lead))

    def params(cid=None):
        if cid is None:
            return pltpu.CompilerParams(vmem_limit_bytes=VLIMIT)
        return pltpu.CompilerParams(vmem_limit_bytes=VLIMIT, collective_id=cid, has_side_effects=True)

    x_all, x_pts, w_all, n0, n2 = pl.pallas_call(
        functools.partial(up_kernel, rows, cols),
        out_shape=(shape(rows, packs), shape(3, packs), shape(cols, 2, packs), shape(cols), shape(rows)),
        in_specs=[VMEM] * 9,
        out_specs=(VMEM,) * 5,
        scratch_shapes=[
            sems(cols - 1),
            sems(rows - 1),
            sems(deep - 1),
            sems(deep, inner - 1),
            sems(2),
            sems(cols - 1),
        ],
        compiler_params=params(0),
    )(x_vectors, w_vectors, order2, vbasis, ubasis, leaf_up_v, leaf_up_u, transfer_u, transfer_v)
    tiles = near_pairs[1] // leaves // cols
    ids = jnp.concatenate(
        [
            coupling_pairs[0] - row_base,
            coupling_pairs[1] // leaves // cols * leaves + coupling_pairs[1] % leaves,
            near_pairs[0] - row_base,
            (tiles - my_row + rows + 1) % rows * leaves + near_pairs[1] % leaves,
            coupling_count,
        ]
    )
    y_part, z_part, n_part = pl.pallas_call(
        slot_kernel,
        out_shape=(shape(cols, 2, packs), shape(rows, packs), shape(3, packs)),
        in_specs=[SMEM] + [VMEM] * 5,
        out_specs=(VMEM,) * 3,
        scratch_shapes=[
            buf(rows * leaves),
            buf(3 * leaves),
            buf(cols * leaves),
            buf(cols * leaves),
            buf(cols * leaves, dtype=F32),
            buf(cols * leaves, dtype=F32),
            buf(rows * leaves, dtype=F32),
            buf(3 * leaves, dtype=F32),
        ],
        compiler_params=params(),
    )(ids, x_all, x_pts, w_all, coupling, near_blocks)
    return pl.pallas_call(
        functools.partial(down_kernel, rows, cols),
        out_shape=(jax.ShapeDtypeStruct((q, piece), BF),) * 2,
        in_specs=[VMEM] * 13,
        out_specs=(VMEM,) * 2,
        scratch_shapes=[
            buf(cols - 1, 2, packs),
            buf(deep, inner - 1, packs),
            buf(deep - 1, packs),
            buf(deep - 1, packs),
            buf(2, packs),
            buf(2 * (rows + cols), dtype=F32),
            sems(cols - 1),
            sems(deep, inner - 1),
            sems(deep - 1),
            sems(2),
        ],
        compiler_params=params(1),
    )(
        y_part, z_part, n_part, n0, n2, order2, ubasis, vbasis, leaf_up_u, leaf_up_v,
        transfer_u, transfer_v, upper_coupling,
    )


def solution(mesh):
    both = P(None, ("row", "col"))
    flat = P(("row", "col"))
    return jax.shard_map(
        per_device,
        mesh=mesh,
        in_specs=(both, both, flat, both, both, both, both, both, both, flat, both, both, P(), P(), P()),
        out_specs=(both, both),
        check_vma=False,
    )
```

```python
import functools

import jax
import jax.numpy as jnp
from jax import lax
from jax.experimental import pallas as pl
from jax.experimental.pallas import tpu as pltpu
from jax.sharding import PartitionSpec as P

BF = jnp.bfloat16
F32 = jnp.float32
VMEM = pl.BlockSpec(memory_space=pltpu.VMEM)
SMEM = pl.BlockSpec(memory_space=pltpu.SMEM)
NN = (((1,), (0,)), ((), ()))
NT = (((1,), (1,)), ((), ()))


def mm(a, b, dims=NN):
    return lax.dot_general(a, b, dims, preferred_element_type=F32)


def left_mask(half, dtype):
    lane = lax.broadcasted_iota(jnp.int32, (1, 2 * half), 1)
    return (lane < half).astype(F32).astype(dtype), (lane >= half).astype(F32).astype(dtype)


def diag2(v, ml, mr):
    return jnp.concatenate([v * ml, v * mr], axis=0)


def swap2(a, b, isl, half):
    return jnp.where(isl, a, pltpu.roll(b, half, 1)), jnp.where(isl, pltpu.roll(a, half, 1), b)


def split_leaves(v, isl, half):
    h = v.shape[0] // 2
    return swap2(v[:h], v[h:], isl, half)


def join_leaves(a, b, isl, half):
    return jnp.concatenate(swap2(a, b, isl, half), axis=0)


def quot(v, n):
    return lax.shift_right_logical(v, n.bit_length() - 1) if n & (n - 1) == 0 else lax.div(v, n)


def mod(v, n):
    return lax.bitwise_and(v, n - 1) if n & (n - 1) == 0 else lax.rem(v, n)


def split2(v):
    hi = v.astype(BF)
    return hi, (v - hi.astype(F32)).astype(BF)


def mm2(v, b, dims):
    hi, lo = split2(v)
    return mm(hi, b, dims) + mm(lo, b, dims)


def one_hot(order_ref, base):
    n = order_ref.shape[1]
    src = lax.broadcasted_iota(jnp.int32, (n, n), 0)
    return jnp.where(src == order_ref[...] - base, 1.0, 0.0).astype(BF)


def grid_of(rows):
    inner = 1 << ((rows.bit_length() - 1) // 2)
    return rows // inner, inner


def greet(rows, cols, r, c):
    bar = pltpu.get_barrier_semaphore()
    for d in range(1, rows):
        pl.semaphore_signal(bar, inc=1, device_id={"row": lax.rem(r + d, rows)}, device_id_type=pl.DeviceIdType.MESH)
    for d in range(1, cols):
        pl.semaphore_signal(bar, inc=1, device_id={"col": lax.rem(c + d, cols)}, device_id_type=pl.DeviceIdType.MESH)
    return bar


def push(src, dst, sems, at, axis, peer):
    copy = pltpu.make_async_remote_copy(
        src_ref=src,
        dst_ref=dst,
        send_sem=sems.at[(0, *at)],
        recv_sem=sems.at[(1, *at)],
        device_id={axis: peer},
        device_id_type=pl.DeviceIdType.MESH,
    )
    copy.start()
    return copy


def chunk_at(ref, at, wide):
    return ref[:, pl.ds(pl.multiple_of(at * wide, wide), wide)]


def combine(v0, v1, fv, fu, ml, mr, isl, half):
    xp = jnp.where(isl, v0, pltpu.roll(v1, half, 1)).astype(BF)
    wp = jnp.where(isl, pltpu.roll(v0, half, 1), v1).astype(BF)
    x = mm(xp, diag2(fv, ml, mr))
    w = mm(wp, diag2(fu, ml, mr))
    return jnp.where(isl, x + pltpu.roll(x, half, 1), w + pltpu.roll(w, half, 1)).astype(BF)


def up_kernel(rows, cols, x_ref, w_ref, order_ref, v_ref, u_ref, ev_ref, eu_ref, fu_ref, fv_ref,
              xc_ref, xp_ref, wa_ref, n0_ref, n2_ref, na_sem, nb_sem, z_sem, x_sem, p_sem, w_sem):
    q, n = x_ref.shape
    packs = xc_ref.shape[1] // 2
    wide = xc_ref.shape[3]
    half = wide // 2
    deep, inner = grid_of(rows)
    r = lax.axis_index("row")
    c = lax.axis_index("col")
    zi = r // inner
    xi = lax.rem(r, inner)
    bar = greet(rows, cols, r, c)
    ml, mr = left_mask(half, BF)
    isl = lax.broadcasted_iota(jnp.int32, (q, wide), 1) < half
    hot = one_hot(order_ref, (r * cols + c) * n)
    low = lax.broadcasted_iota(jnp.int32, (q // 2, wide), 1) < half
    both = mm(jnp.concatenate([x_ref[...], w_ref[...]], axis=0), hot)
    folds = []
    for side, (b_ref, e_ref) in enumerate(((v_ref, ev_ref), (u_ref, eu_ref))):
        pts = both[side * q:(side + 1) * q].astype(BF)
        node = jnp.zeros((q, wide), F32)
        for m in range(packs):
            cs = slice(m * wide, (m + 1) * wide)
            pm = pts[:, cs]
            cf = mm(pm, diag2(b_ref[:, cs], ml, mr), NT)
            cm = cf.astype(BF)
            c_leaves = split_leaves(cf, low, half)
            p_leaves = split_leaves(both[side * q:(side + 1) * q, cs], low, half)
            for e in range(2):
                ce, pe = c_leaves[e].astype(BF), p_leaves[e].astype(BF)
                if side == 0:
                    xc_ref[r, 2 * m + e] = ce
                    xp_ref[1, 2 * m + e] = pe
                else:
                    wa_ref[c, 0, 2 * m + e] = ce
                    wa_ref[c, 1, 2 * m + e] = pe
            node = node + mm(cm, diag2(e_ref[:, cs], ml, mr))
        folds.append(node + pltpu.roll(node, half, 1))
    n0_ref[c] = jnp.where(isl, folds[0], folds[1]).astype(BF)
    pl.semaphore_wait(bar, rows + cols - 2)
    node_a = [
        push(n0_ref.at[c], n0_ref.at[c], na_sem, (d - 1,), "col", lax.rem(c + d, cols)) for d in range(1, cols)
    ]
    own = xc_ref.at[r]
    along = [
        push(own, own, z_sem, (d - 1,), "row", lax.rem(zi + d, deep) * inner + xi) for d in range(1, deep)
    ]
    across = [
        push(own, own, x_sem, (0, d - 1), "row", zi * inner + lax.rem(xi + d, inner)) for d in range(1, inner)
    ]
    points = [
        push(xp_ref.at[1], xp_ref.at[0], p_sem, (0,), "row", lax.rem(r + 1, rows)),
        push(xp_ref.at[1], xp_ref.at[2], p_sem, (1,), "row", lax.rem(r + rows - 1, rows)),
    ]
    wide_w = [
        push(wa_ref.at[c], wa_ref.at[c], w_sem, (d - 1,), "col", lax.rem(c + d, cols)) for d in range(1, cols)
    ]
    for copy in node_a:
        copy.wait_recv()
    dev_count = rows * cols
    vals = [n0_ref[i].astype(F32) for i in range(cols)]
    level = 0
    while len(vals) > 1:
        off = dev_count - (dev_count >> level)
        count = len(vals) // 2
        nxt = []
        for i in range(count):
            at = off + r * count + i
            nxt.append(
                combine(vals[2 * i], vals[2 * i + 1], chunk_at(fv_ref, at, wide), chunk_at(fu_ref, at, wide), ml, mr, isl, half)
            )
        vals = [v.astype(F32) for v in nxt]
        level += 1
    n2_ref[r] = vals[0].astype(BF)
    node_b = [
        push(n2_ref.at[r], n2_ref.at[r], nb_sem, (d - 1,), "row", lax.rem(r + d, rows)) for d in range(1, rows)
    ]
    for d in range(1, deep):
        along[d - 1].wait_recv()
        got = xc_ref.at[lax.rem(zi + deep - d, deep) * inner + xi]
        across += [
            push(got, got, x_sem, (d, e - 1), "row", zi * inner + lax.rem(xi + e, inner)) for e in range(1, inner)
        ]
    for copy in node_b + across + points + wide_w:
        copy.wait_recv()
    for copy in node_a + node_b + along + across + points + wide_w:
        copy.wait_send()


def slot_kernel(rows, cols, cp_ref, np_ref, live_ref, x_ref, p_ref, w_ref, s_ref, d_ref, y_ref, z_ref, n_ref, ya, zc, zn):
    leaves, _, wide = x_ref.shape[1:]
    half = wide // 2
    ml, mr = left_mask(half, BF)
    slots = cp_ref.shape[1]
    nears = np_ref.shape[1]
    live = live_ref[0]
    my_row = lax.axis_index("row")
    row_base = my_row * cols * leaves
    lane = lax.broadcasted_iota(jnp.int32, (1, wide), 1)

    def clear(acc):
        def one(i, carry):
            acc[i] = jnp.zeros(acc.shape[1:], F32)
            return carry
        lax.fori_loop(0, acc.shape[0], one, 0)

    clear(ya.at[0])
    clear(ya.at[1])
    clear(zc)
    clear(zn)

    def run(pairs, mat, kind, first, last, unroll, masked):
        near = kind == 1

        def step(g, carry):
            work = []
            for k in range(unroll):
                p = g * unroll + k
                blk = mat[:, pl.ds(pl.multiple_of(p * wide, wide), wide)]
                alt = jnp.concatenate([blk[:, half:], blk[:, :half]], axis=1)
                for e in range(2):
                    b = 2 * p + e
                    i = pairs[0, b] - row_base
                    l = pairs[1, b]
                    group = quot(l, cols * leaves)
                    leaf = mod(l, leaves)
                    if near:
                        group = mod(group - my_row + (rows + 1), rows)
                    a_l, a_r = ml, mr
                    if masked:
                        ok = jnp.where(b < live, 1.0, 0.0)
                        a_l = jnp.where(lane < half, ok, 0.0).astype(BF)
                        a_r = jnp.where(lane < half, 0.0, ok).astype(BF)
                    one, two = (alt, blk) if e else (blk, alt)
                    both = jnp.concatenate([one * a_l, two * a_r], axis=0)
                    xv = p_ref[group, leaf] if near else x_ref[group, leaf]
                    wv = w_ref[quot(i, leaves), kind, mod(i, leaves)]
                    j = group * leaves + leaf
                    work.append((i, j, mm(xv, both, NT), mm(wv, both)))
            zacc = zn if near else zc
            for i, j, yv, zv in work:
                ya[kind, i] += yv
                zacc[j] += zv
            return carry
        lax.fori_loop(first, last, step, 0)

    unroll = 4
    full = quot(live, 2 * unroll)
    run(cp_ref, s_ref, 0, 0, full, unroll, False)
    run(cp_ref, s_ref, 0, full, quot(live + 2 * unroll - 1, 2 * unroll), unroll, True)
    run(np_ref, d_ref, 1, 0, nears // (2 * unroll), unroll, False)

    def out_y(i, carry):
        for t in range(2):
            for m in range(leaves):
                y_ref[i, t, m] = ya[t, i * leaves + m].astype(BF)
        return carry

    def out_z(i, carry):
        for m in range(leaves):
            z_ref[i, m] = zc[i * leaves + m].astype(BF)
        return carry

    def out_n(i, carry):
        for m in range(leaves):
            n_ref[i, m] = zn[i * leaves + m].astype(BF)
        return carry

    lax.fori_loop(0, cols, out_y, 0)
    lax.fori_loop(0, rows, out_z, 0)
    lax.fori_loop(0, 3, out_n, 0)


def down_kernel(rows, cols, y_ref, z_ref, n_ref, n0_ref, n2_ref, order_ref, u_ref, v_ref, eu_ref, ev_ref, fu_ref, fv_ref,
                s_ref, o_ref, y_in, z1_in, z1_out, z2_in, zn_in, nodes, y_sem, z1_sem, z2_sem, n_sem):
    _, leaves, q, wide = z_ref.shape
    q = 2 * q
    half = wide // 2
    low = lax.broadcasted_iota(jnp.int32, (q // 2, wide), 1) < half
    deep, inner = grid_of(rows)
    dev_count = rows * cols
    r = lax.axis_index("row")
    c = lax.axis_index("col")
    me = r * cols + c
    zi = r // inner
    xi = lax.rem(r, inner)
    bar = greet(rows, cols, r, c)
    ml, mr = left_mask(half, BF)
    isl = lax.broadcasted_iota(jnp.int32, (q, wide), 1) < half
    hot = one_hot(order_ref, me * order_ref.shape[1])
    pl.semaphore_wait(bar, rows + cols - 2)
    first = {}
    for d in list(range(1, deep)) + [0]:
        to = lax.rem(zi + d, deep) * inner
        first[d] = []
        for e in range(1, inner):
            peer = lax.rem(xi + e, inner)
            first[d].append(
                push(z_ref.at[to + peer], z1_in.at[d, e - 1], z1_sem, (d, e - 1), "row", zi * inner + peer)
            )
    near = [
        push(n_ref.at[0], zn_in.at[0], n_sem, (0,), "row", lax.rem(r + rows - 1, rows)),
        push(n_ref.at[2], zn_in.at[1], n_sem, (1,), "row", lax.rem(r + 1, rows)),
    ]
    y_copies = []
    for d in range(1, cols):
        peer = lax.rem(c + d, cols)
        y_copies.append(push(y_ref.at[peer], y_in.at[d - 1], y_sem, (d - 1,), "col", peer))

    second = []
    for d in range(1, deep):
        for copy in first[d]:
            copy.wait_recv()
        to = lax.rem(zi + d, deep) * inner + xi
        for m in range(leaves):
            total = z_ref[to, m].astype(F32)
            for e in range(inner - 1):
                total = total + z1_in[d, e, m].astype(F32)
            z1_out[d - 1, m] = total.astype(BF)
        second.append(push(z1_out.at[d - 1], z2_in.at[d - 1], z2_sem, (d - 1,), "row", to))

    levels = dev_count.bit_length() - 1
    starts = []
    at = 0
    vals = None
    for level in range(levels):
        if level == 0:
            vals = [n0_ref[i].astype(F32) for i in range(cols)]
            split = r
        elif cols >> level == 1:
            vals = [n2_ref[i].astype(F32) for i in range(rows)]
            split = 0
        starts.append((at, c >> level if cols >> level > 1 else me >> level))
        for i, v in enumerate(vals):
            nodes[at + i] = v
        at += len(vals)
        off = dev_count - (dev_count >> level)
        count = len(vals) // 2
        if level < levels - 1 and count * 2 == len(vals) and not (cols >> level == 2):
            vals = [
                combine(
                    vals[2 * i],
                    vals[2 * i + 1],
                    chunk_at(fv_ref, off + split * count + i, wide),
                    chunk_at(fu_ref, off + split * count + i, wide),
                    ml, mr, isl, half,
                ).astype(F32)
                for i in range(count)
            ]

    lane_half = (lax.broadcasted_iota(jnp.int32, (q, wide), 1) >= half).astype(jnp.int32)

    def turned(v, chunk, side):
        return mm2(jnp.where(lane_half == side, v, 0.0), jnp.concatenate([chunk, chunk], axis=0), NT)

    y_down = z_down = None
    for level in range(levels - 1, -1, -1):
        start, local = starts[level]
        own = me >> level
        side = lax.rem(own, 2)
        sib = nodes[start + local + 1 - 2 * lax.rem(local, 2)]
        rolled = pltpu.roll(sib, half, 1)
        xs = jnp.where(isl, sib, rolled)
        ws = jnp.where(isl, rolled, 0.0).astype(BF)
        at = dev_count - (dev_count >> level) + own // 2
        cup = chunk_at(s_ref, at, wide)
        dup = jnp.concatenate([cup, cup], axis=0)
        y_term = mm(jnp.where(lane_half == side, xs, 0.0).astype(BF), dup, NT)
        z_raw = jnp.where(lane_half == 1 - side, mm(ws, dup), 0.0)
        z_term = z_raw + pltpu.roll(z_raw, half, 1)
        if level < levels - 1:
            y_term = y_term + turned(y_down, chunk_at(fu_ref, at, wide), side)
            z_term = z_term + turned(z_down, chunk_at(fv_ref, at, wide), side)
        y_down, z_down = y_term, z_term

    perms = []
    for flip, (down, b_ref, e_ref) in enumerate(((y_down, u_ref, eu_ref), (z_down, v_ref, ev_ref))):
        if flip == 0:
            for copy in y_copies:
                copy.wait_recv()
        else:
            for copy in first[0] + second + near:
                copy.wait_recv()
        parts = []
        for m in range(leaves // 2):
            cs = slice(m * wide, (m + 1) * wide)
            sums = []
            for n in (2 * m, 2 * m + 1):
                if flip == 0:
                    coef, raw = y_ref[c, 0, n].astype(F32), y_ref[c, 1, n].astype(F32)
                    for d in range(cols - 1):
                        coef = coef + y_in[d, 0, n].astype(F32)
                        raw = raw + y_in[d, 1, n].astype(F32)
                else:
                    coef, raw = z_ref[r, n].astype(F32), n_ref[1, n].astype(F32)
                    for e in range(inner - 1):
                        coef = coef + z1_in[0, e, n].astype(F32)
                    for d in range(deep - 1):
                        coef = coef + z2_in[d, n].astype(F32)
                    for k in range(2):
                        raw = raw + zn_in[k, n].astype(F32)
                sums.append((coef, raw))
            coef, raw = (join_leaves(a, b, low, half) for a, b in zip(*sums))
            leaf = (coef + mm2(down, diag2(e_ref[:, cs], ml, mr), NT)).astype(BF)
            parts.append((mm(leaf, diag2(b_ref[:, cs], ml, mr)) + raw).astype(BF))
        perms.append(jnp.concatenate(parts, axis=1))
    o_ref[...] = mm(jnp.concatenate(perms, axis=0), hot, NT).astype(BF)
    for copies in (*first.values(), second, near, y_copies):
        for copy in copies:
            copy.wait_send()


def per_device(
    x_vectors,
    w_vectors,
    order,
    ubasis,
    vbasis,
    leaf_up_u,
    leaf_up_v,
    coupling,
    coupling_pairs,
    coupling_count,
    near_blocks,
    near_pairs,
    transfer_u,
    transfer_v,
    upper_coupling,
):
    q, piece = x_vectors.shape
    rank = ubasis.shape[0]
    leaves = leaf_up_u.shape[1] // rank
    wide = 2 * rank
    rows = lax.axis_size("row")
    cols = lax.axis_size("col")
    deep, inner = grid_of(rows)
    order2 = order.reshape(1, piece)

    def leaf_shape(*lead):
        return jax.ShapeDtypeStruct((*lead, q // 2, wide), BF)

    def shape(*lead):
        return jax.ShapeDtypeStruct((*lead, q, wide), BF)

    def leaf_buf(*lead, dtype=BF):
        return pltpu.VMEM((*lead, q // 2, wide), dtype)

    def buf(*lead, dtype=BF):
        return pltpu.VMEM((*lead, q, wide), dtype)

    def sems(*lead):
        return pltpu.SemaphoreType.DMA((2, *lead))

    def params(cid=None):
        if cid is None:
            return pltpu.CompilerParams(vmem_limit_bytes=28 * 1024 * 1024)
        return pltpu.CompilerParams(vmem_limit_bytes=24 * 1024 * 1024, collective_id=cid, has_side_effects=True)

    cost = pl.CostEstimate(
        flops=12 * q * rank * coupling.shape[1], bytes_accessed=128 * q * piece * rows, transcendentals=0
    )
    x_all, x_pts, w_all, n0, n2 = pl.pallas_call(
        functools.partial(up_kernel, rows, cols),
        out_shape=(leaf_shape(rows, leaves), leaf_shape(3, leaves), leaf_shape(cols, 2, leaves), shape(cols), shape(rows)),
        in_specs=[VMEM] * 9,
        out_specs=(VMEM,) * 5,
        scratch_shapes=[
            sems(cols - 1),
            sems(rows - 1),
            sems(deep - 1),
            sems(deep, inner - 1),
            sems(2),
            sems(cols - 1),
        ],
        compiler_params=params(0),
        cost_estimate=cost,
    )(x_vectors, w_vectors, order2, vbasis, ubasis, leaf_up_v, leaf_up_u, transfer_u, transfer_v)
    y_part, z_part, n_part = pl.pallas_call(
        functools.partial(slot_kernel, rows, cols),
        out_shape=(leaf_shape(cols, 2, leaves), leaf_shape(rows, leaves), leaf_shape(3, leaves)),
        in_specs=[SMEM] * 3 + [VMEM] * 5,
        out_specs=(VMEM,) * 3,
        scratch_shapes=[
            leaf_buf(2, cols * leaves, dtype=F32),
            leaf_buf(rows * leaves, dtype=F32),
            leaf_buf(3 * leaves, dtype=F32),
        ],
        compiler_params=params(),
        cost_estimate=cost,
    )(coupling_pairs, near_pairs, coupling_count, x_all, x_pts, w_all, coupling, near_blocks)
    out = pl.pallas_call(
        functools.partial(down_kernel, rows, cols),
        out_shape=jax.ShapeDtypeStruct((2 * q, piece), BF),
        in_specs=[VMEM] * 13,
        out_specs=VMEM,
        scratch_shapes=[
            leaf_buf(cols - 1, 2, leaves),
            leaf_buf(deep, inner - 1, leaves),
            leaf_buf(deep - 1, leaves),
            leaf_buf(deep - 1, leaves),
            leaf_buf(2, leaves),
            buf(2 * (rows + cols), dtype=F32),
            sems(cols - 1),
            sems(deep, inner - 1),
            sems(deep - 1),
            sems(2),
        ],
        compiler_params=params(1),
        cost_estimate=cost,
    )(
        y_part, z_part, n_part, n0, n2, order2, ubasis, vbasis, leaf_up_u, leaf_up_v,
        transfer_u, transfer_v, upper_coupling,
    )
    return out[:q], out[q:]


def solution(mesh):
    both = P(None, ("row", "col"))
    flat = P(("row", "col"))
    return jax.shard_map(
        per_device,
        mesh=mesh,
        in_specs=(both, both, flat, both, both, both, both, both, both, flat, both, both, P(), P(), P()),
        out_specs=(both, both),
        check_vma=False,
    )
```

```python
import functools

import jax
import jax.numpy as jnp
from jax import lax
from jax.experimental import pallas as pl
from jax.experimental.pallas import tpu as pltpu
from jax.sharding import PartitionSpec as P

BF = jnp.bfloat16
F32 = jnp.float32
VMEM = pl.BlockSpec(memory_space=pltpu.VMEM)
SMEM = pl.BlockSpec(memory_space=pltpu.SMEM)
NN = (((1,), (0,)), ((), ()))
NT = (((1,), (1,)), ((), ()))
VLIMIT = 60 * 1024 * 1024


def mm(a, b, dims=NN):
    return lax.dot_general(a, b, dims, preferred_element_type=F32)


def left_mask(half, dtype):
    lane = lax.broadcasted_iota(jnp.int32, (1, 2 * half), 1)
    return (lane < half).astype(F32).astype(dtype), (lane >= half).astype(F32).astype(dtype)


def diag2(v, ml, mr):
    return jnp.concatenate([v * ml, v * mr], axis=0)


def quot(v, n):
    return lax.shift_right_logical(v, n.bit_length() - 1) if n & (n - 1) == 0 else lax.div(v, n)


def mod(v, n):
    return lax.bitwise_and(v, n - 1) if n & (n - 1) == 0 else lax.rem(v, n)


def split2(v):
    hi = v.astype(BF)
    return hi, (v - hi.astype(F32)).astype(BF)


def mm2(v, b, dims):
    hi, lo = split2(v)
    return mm(hi, b, dims) + mm(lo, b, dims)


def one_hot(order_ref, base):
    n = order_ref.shape[1]
    src = lax.broadcasted_iota(jnp.int32, (n, n), 0)
    return jnp.where(src == order_ref[...] - base, 1.0, 0.0).astype(BF)


def grid_of(rows):
    inner = 1 << ((rows.bit_length() - 1) // 2)
    return rows // inner, inner


def greet(rows, cols, r, c):
    bar = pltpu.get_barrier_semaphore()
    for d in range(1, rows):
        pl.semaphore_signal(bar, inc=1, device_id={"row": lax.rem(r + d, rows)}, device_id_type=pl.DeviceIdType.MESH)
    for d in range(1, cols):
        pl.semaphore_signal(bar, inc=1, device_id={"col": lax.rem(c + d, cols)}, device_id_type=pl.DeviceIdType.MESH)
    return bar


def push(src, dst, sems, at, axis, peer):
    copy = pltpu.make_async_remote_copy(
        src_ref=src,
        dst_ref=dst,
        send_sem=sems.at[(0, *at)],
        recv_sem=sems.at[(1, *at)],
        device_id={axis: peer},
        device_id_type=pl.DeviceIdType.MESH,
    )
    copy.start()
    return copy


def chunk_at(ref, at, wide):
    return ref[:, pl.ds(pl.multiple_of(at * wide, wide), wide)]


def combine(v0, v1, fv, fu, ml, mr, isl, half):
    xp = jnp.where(isl, v0, pltpu.roll(v1, half, 1)).astype(BF)
    wp = jnp.where(isl, pltpu.roll(v0, half, 1), v1).astype(BF)
    x = mm(xp, diag2(fv, ml, mr))
    w = mm(wp, diag2(fu, ml, mr))
    return jnp.where(isl, x + pltpu.roll(x, half, 1), w + pltpu.roll(w, half, 1)).astype(BF)


def up_kernel(rows, cols, x_ref, w_ref, order_ref, v_ref, u_ref, ev_ref, eu_ref, fu_ref, fv_ref,
              xc_ref, xp_ref, wa_ref, n0_ref, n2_ref, na_sem, nb_sem, z_sem, x_sem, p_sem, w_sem):
    q, n = x_ref.shape
    packs = xc_ref.shape[1]
    wide = xc_ref.shape[3]
    half = wide // 2
    deep, inner = grid_of(rows)
    r = lax.axis_index("row")
    c = lax.axis_index("col")
    zi = r // inner
    xi = lax.rem(r, inner)
    bar = greet(rows, cols, r, c)
    ml, mr = left_mask(half, BF)
    isl = lax.broadcasted_iota(jnp.int32, (q, wide), 1) < half
    hot = one_hot(order_ref, (r * cols + c) * n)
    both = mm(jnp.concatenate([x_ref[...], w_ref[...]], axis=0), hot).astype(BF)
    folds = []
    for side, (b_ref, e_ref) in enumerate(((v_ref, ev_ref), (u_ref, eu_ref))):
        pts = both[side * q:(side + 1) * q]
        node = jnp.zeros((q, wide), F32)
        for m in range(packs):
            cs = slice(m * wide, (m + 1) * wide)
            pm = pts[:, cs]
            cm = mm(pm, diag2(b_ref[:, cs], ml, mr), NT).astype(BF)
            if side == 0:
                xc_ref[r, m] = cm
                xp_ref[1, m] = pm
            else:
                wa_ref[c, 0, m] = cm
                wa_ref[c, 1, m] = pm
            node = node + mm(cm, diag2(e_ref[:, cs], ml, mr))
        folds.append(node + pltpu.roll(node, half, 1))
    n0_ref[c] = jnp.where(isl, folds[0], folds[1]).astype(BF)
    pl.semaphore_wait(bar, rows + cols - 2)
    node_a = [
        push(n0_ref.at[c], n0_ref.at[c], na_sem, (d - 1,), "col", lax.rem(c + d, cols)) for d in range(1, cols)
    ]
    own = xc_ref.at[r]
    along = [
        push(own, own, z_sem, (d - 1,), "row", lax.rem(zi + d, deep) * inner + xi) for d in range(1, deep)
    ]
    across = [
        push(own, own, x_sem, (0, d - 1), "row", zi * inner + lax.rem(xi + d, inner)) for d in range(1, inner)
    ]
    points = [
        push(xp_ref.at[1], xp_ref.at[0], p_sem, (0,), "row", lax.rem(r + 1, rows)),
        push(xp_ref.at[1], xp_ref.at[2], p_sem, (1,), "row", lax.rem(r + rows - 1, rows)),
    ]
    wide_w = [
        push(wa_ref.at[c], wa_ref.at[c], w_sem, (d - 1,), "col", lax.rem(c + d, cols)) for d in range(1, cols)
    ]
    for copy in node_a:
        copy.wait_recv()
    dev_count = rows * cols
    vals = [n0_ref[i].astype(F32) for i in range(cols)]
    level = 0
    while len(vals) > 1:
        off = dev_count - (dev_count >> level)
        count = len(vals) // 2
        nxt = []
        for i in range(count):
            at = off + r * count + i
            nxt.append(
                combine(vals[2 * i], vals[2 * i + 1], chunk_at(fv_ref, at, wide), chunk_at(fu_ref, at, wide), ml, mr, isl, half)
            )
        vals = [v.astype(F32) for v in nxt]
        level += 1
    n2_ref[r] = vals[0].astype(BF)
    node_b = [
        push(n2_ref.at[r], n2_ref.at[r], nb_sem, (d - 1,), "row", lax.rem(r + d, rows)) for d in range(1, rows)
    ]
    for d in range(1, deep):
        along[d - 1].wait_recv()
        got = xc_ref.at[lax.rem(zi + deep - d, deep) * inner + xi]
        across += [
            push(got, got, x_sem, (d, e - 1), "row", zi * inner + lax.rem(xi + e, inner)) for e in range(1, inner)
        ]
    for copy in node_b + across + points + wide_w:
        copy.wait_recv()
    for copy in node_a + node_b + along + across + points + wide_w:
        copy.wait_send()


def slot_kernel(cp_ref, np_ref, live_ref, x_ref, p_ref, w_ref, s_ref, d_ref, y_ref, z_ref, n_ref, xc, xp, wc, wp, yc, yn, zc, zn):
    rows, packs, q, wide = x_ref.shape
    cols = w_ref.shape[0]
    half = wide // 2
    ml, mr = left_mask(half, BF)
    leaves = 2 * packs
    nears = np_ref.shape[1]
    live = live_ref[0]
    my_row = lax.axis_index("row")
    row_base = my_row * cols * leaves
    isl = lax.broadcasted_iota(jnp.int32, (q, wide), 1) < half
    lane = lax.broadcasted_iota(jnp.int32, (1, wide), 1)
    for acc in (yc, yn, zc, zn):
        def clear(i, carry, acc=acc):
            acc[i] = jnp.zeros(acc.shape[1:], F32)
            return carry
        lax.fori_loop(0, acc.shape[0], clear, 0)

    def widen(src, table, at):
        v = src[...]
        r = jnp.concatenate([v[:, half:], v[:, :half]], axis=1)
        table[at] = v * ml + r * mr
        table[at + 1] = r * ml + v * mr

    def fill_x(i, carry):
        for m in range(packs):
            widen(x_ref.at[i, m], xc, 2 * (i * packs + m))
        return carry

    def fill_w(i, carry):
        for m in range(packs):
            widen(w_ref.at[i, 0, m], wc, 2 * (i * packs + m))
            widen(w_ref.at[i, 1, m], wp, 2 * (i * packs + m))
        return carry

    lax.fori_loop(0, rows, fill_x, 0)
    lax.fori_loop(0, cols, fill_w, 0)
    for k in range(3):
        for m in range(packs):
            widen(p_ref.at[k, m], xp, 2 * (k * packs + m))

    def place(pairs, b, near):
        leaf = pairs[1, b]
        group = quot(leaf, cols * leaves)
        if near:
            group = mod(group - my_row + (rows + 1), rows)
        return pairs[0, b] - row_base, group * leaves + mod(leaf, leaves)

    def run(pairs, mat, xt, wt, ya, za, near, masked, first, last, unroll):
        def step(g, carry):
            work = []
            for k in range(unroll):
                p = g * unroll + k
                i0, j0 = place(pairs, 2 * p, near)
                i1, j1 = place(pairs, 2 * p + 1, near)
                blk = mat[:, pl.ds(pl.multiple_of(p * wide, wide), wide)]
                if masked:
                    left_ok = jnp.where(2 * p < live, 1.0, 0.0)
                    right_ok = jnp.where(2 * p + 1 < live, 1.0, 0.0)
                    a = jnp.where(lane < half, left_ok, 0.0).astype(BF)
                    b = jnp.where(lane < half, 0.0, right_ok).astype(BF)
                else:
                    a, b = ml, mr
                pair = jnp.concatenate([blk * a, blk * b], axis=0)
                xs = xt[j0] * ml + xt[j1] * mr
                ws = wt[i0] * ml + wt[i1] * mr
                work.append((i0, i1, j0, j1, mm(xs, pair, NT), mm(ws, pair)))
            for i0, i1, j0, j1, yv, zv in work:
                ya[i0] += jnp.where(isl, yv, 0.0)
                ya[i1] += jnp.where(isl, 0.0, yv)
                za[j0] += jnp.where(isl, zv, 0.0)
                za[j1] += jnp.where(isl, 0.0, zv)
            return carry
        lax.fori_loop(first, last, step, 0)

    unroll = 4
    full = quot(live, 2 * unroll)
    most = quot(live + 2 * unroll - 1, 2 * unroll)
    run(cp_ref, s_ref, xc, wc, yc, zc, False, False, 0, full, unroll)
    run(cp_ref, s_ref, xc, wc, yc, zc, False, True, full, most, unroll)
    run(np_ref, d_ref, xp, wp, yn, zn, True, False, 0, nears // (2 * unroll), unroll)

    def fold(acc, at):
        a, b = acc[at], acc[at + 1]
        return jnp.where(isl, a + pltpu.roll(a, half, 1), b + pltpu.roll(b, half, 1))

    def out_y(i, carry):
        for m in range(packs):
            y_ref[i, 0, m] = fold(yc, 2 * (i * packs + m)).astype(y_ref.dtype)
            y_ref[i, 1, m] = fold(yn, 2 * (i * packs + m)).astype(y_ref.dtype)
        return carry

    def out_z(i, carry):
        for m in range(packs):
            z_ref[i, m] = fold(zc, 2 * (i * packs + m)).astype(z_ref.dtype)
        return carry

    def out_n(i, carry):
        for m in range(packs):
            n_ref[i, m] = fold(zn, 2 * (i * packs + m)).astype(n_ref.dtype)
        return carry

    lax.fori_loop(0, cols, out_y, 0)
    lax.fori_loop(0, rows, out_z, 0)
    lax.fori_loop(0, 3, out_n, 0)


def down_kernel(rows, cols, y_ref, z_ref, n_ref, n0_ref, n2_ref, order_ref, u_ref, v_ref, eu_ref, ev_ref, fu_ref, fv_ref,
                s_ref, o_ref, y_in, z1_in, z1_out, z2_in, zn_in, nodes, y_sem, z1_sem, z2_sem, n_sem):
    _, packs, q, wide = z_ref.shape
    half = wide // 2
    deep, inner = grid_of(rows)
    dev_count = rows * cols
    r = lax.axis_index("row")
    c = lax.axis_index("col")
    me = r * cols + c
    zi = r // inner
    xi = lax.rem(r, inner)
    bar = greet(rows, cols, r, c)
    ml, mr = left_mask(half, BF)
    isl = lax.broadcasted_iota(jnp.int32, (q, wide), 1) < half
    hot = one_hot(order_ref, me * order_ref.shape[1])
    pl.semaphore_wait(bar, rows + cols - 2)
    first = {}
    for d in list(range(1, deep)) + [0]:
        to = lax.rem(zi + d, deep) * inner
        first[d] = []
        for e in range(1, inner):
            peer = lax.rem(xi + e, inner)
            first[d].append(
                push(z_ref.at[to + peer], z1_in.at[d, e - 1], z1_sem, (d, e - 1), "row", zi * inner + peer)
            )
    near = [
        push(n_ref.at[0], zn_in.at[0], n_sem, (0,), "row", lax.rem(r + rows - 1, rows)),
        push(n_ref.at[2], zn_in.at[1], n_sem, (1,), "row", lax.rem(r + 1, rows)),
    ]
    y_copies = []
    for d in range(1, cols):
        peer = lax.rem(c + d, cols)
        y_copies.append(push(y_ref.at[peer], y_in.at[d - 1], y_sem, (d - 1,), "col", peer))

    second = []
    for d in range(1, deep):
        for copy in first[d]:
            copy.wait_recv()
        to = lax.rem(zi + d, deep) * inner + xi
        for m in range(packs):
            total = z_ref[to, m].astype(F32)
            for e in range(inner - 1):
                total = total + z1_in[d, e, m].astype(F32)
            z1_out[d - 1, m] = total.astype(BF)
        second.append(push(z1_out.at[d - 1], z2_in.at[d - 1], z2_sem, (d - 1,), "row", to))

    levels = dev_count.bit_length() - 1
    starts = []
    at = 0
    vals = None
    for level in range(levels):
        if level == 0:
            vals = [n0_ref[i].astype(F32) for i in range(cols)]
            split = r
        elif cols >> level == 1:
            vals = [n2_ref[i].astype(F32) for i in range(rows)]
            split = 0
        starts.append((at, c >> level if cols >> level > 1 else me >> level))
        for i, v in enumerate(vals):
            nodes[at + i] = v
        at += len(vals)
        off = dev_count - (dev_count >> level)
        count = len(vals) // 2
        if level < levels - 1 and count * 2 == len(vals) and not (cols >> level == 2):
            vals = [
                combine(
                    vals[2 * i],
                    vals[2 * i + 1],
                    chunk_at(fv_ref, off + split * count + i, wide),
                    chunk_at(fu_ref, off + split * count + i, wide),
                    ml, mr, isl, half,
                ).astype(F32)
                for i in range(count)
            ]

    lane_half = (lax.broadcasted_iota(jnp.int32, (q, wide), 1) >= half).astype(jnp.int32)

    def turned(v, chunk, side):
        return mm2(jnp.where(lane_half == side, v, 0.0), jnp.concatenate([chunk, chunk], axis=0), NT)

    y_down = z_down = None
    for level in range(levels - 1, -1, -1):
        start, local = starts[level]
        own = me >> level
        side = lax.rem(own, 2)
        sib = nodes[start + local + 1 - 2 * lax.rem(local, 2)]
        rolled = pltpu.roll(sib, half, 1)
        xs = jnp.where(isl, sib, rolled)
        ws = jnp.where(isl, rolled, 0.0).astype(BF)
        at = dev_count - (dev_count >> level) + own // 2
        cup = chunk_at(s_ref, at, wide)
        dup = jnp.concatenate([cup, cup], axis=0)
        y_term = mm(jnp.where(lane_half == side, xs, 0.0).astype(BF), dup, NT)
        z_raw = jnp.where(lane_half == 1 - side, mm(ws, dup), 0.0)
        z_term = z_raw + pltpu.roll(z_raw, half, 1)
        if level < levels - 1:
            y_term = y_term + turned(y_down, chunk_at(fu_ref, at, wide), side)
            z_term = z_term + turned(z_down, chunk_at(fv_ref, at, wide), side)
        y_down, z_down = y_term, z_term

    perms = []
    for flip, (down, b_ref, e_ref) in enumerate(((y_down, u_ref, eu_ref), (z_down, v_ref, ev_ref))):
        if flip == 0:
            for copy in y_copies:
                copy.wait_recv()
        else:
            for copy in first[0] + second + near:
                copy.wait_recv()
        parts = []
        for m in range(packs):
            cs = slice(m * wide, (m + 1) * wide)
            if flip == 0:
                coef, raw = y_ref[c, 0, m].astype(F32), y_ref[c, 1, m].astype(F32)
                for d in range(cols - 1):
                    coef = coef + y_in[d, 0, m].astype(F32)
                    raw = raw + y_in[d, 1, m].astype(F32)
            else:
                coef, raw = z_ref[r, m].astype(F32), n_ref[1, m].astype(F32)
                for e in range(inner - 1):
                    coef = coef + z1_in[0, e, m].astype(F32)
                for d in range(deep - 1):
                    coef = coef + z2_in[d, m].astype(F32)
                for k in range(2):
                    raw = raw + zn_in[k, m].astype(F32)
            leaf = (coef + mm2(down, diag2(e_ref[:, cs], ml, mr), NT)).astype(BF)
            parts.append((mm(leaf, diag2(b_ref[:, cs], ml, mr)) + raw).astype(BF))
        perms.append(jnp.concatenate(parts, axis=1))
    o_ref[...] = mm(jnp.concatenate(perms, axis=0), hot, NT).astype(BF)
    for copies in (*first.values(), second, near, y_copies):
        for copy in copies:
            copy.wait_send()


def per_device(
    x_vectors,
    w_vectors,
    order,
    ubasis,
    vbasis,
    leaf_up_u,
    leaf_up_v,
    coupling,
    coupling_pairs,
    coupling_count,
    near_blocks,
    near_pairs,
    transfer_u,
    transfer_v,
    upper_coupling,
):
    q, piece = x_vectors.shape
    rank = ubasis.shape[0]
    leaves = leaf_up_u.shape[1] // rank
    packs = leaves // 2
    wide = 2 * rank
    rows = lax.axis_size("row")
    cols = lax.axis_size("col")
    deep, inner = grid_of(rows)
    order2 = order.reshape(1, piece)

    def shape(*lead):
        return jax.ShapeDtypeStruct((*lead, q, wide), BF)

    def buf(*lead, dtype=BF):
        return pltpu.VMEM((*lead, q, wide), dtype)

    def sems(*lead):
        return pltpu.SemaphoreType.DMA((2, *lead))

    def params(cid=None):
        if cid is None:
            return pltpu.CompilerParams(vmem_limit_bytes=VLIMIT)
        return pltpu.CompilerParams(vmem_limit_bytes=VLIMIT, collective_id=cid, has_side_effects=True)

    x_all, x_pts, w_all, n0, n2 = pl.pallas_call(
        functools.partial(up_kernel, rows, cols),
        out_shape=(shape(rows, packs), shape(3, packs), shape(cols, 2, packs), shape(cols), shape(rows)),
        in_specs=[VMEM] * 9,
        out_specs=(VMEM,) * 5,
        scratch_shapes=[
            sems(cols - 1),
            sems(rows - 1),
            sems(deep - 1),
            sems(deep, inner - 1),
            sems(2),
            sems(cols - 1),
        ],
        compiler_params=params(0),
    )(x_vectors, w_vectors, order2, vbasis, ubasis, leaf_up_v, leaf_up_u, transfer_u, transfer_v)
    y_part, z_part, n_part = pl.pallas_call(
        slot_kernel,
        out_shape=(shape(cols, 2, packs), shape(rows, packs), shape(3, packs)),
        in_specs=[SMEM] * 3 + [VMEM] * 5,
        out_specs=(VMEM,) * 3,
        scratch_shapes=[
            buf(rows * leaves),
            buf(3 * leaves),
            buf(cols * leaves),
            buf(cols * leaves),
            buf(cols * leaves, dtype=F32),
            buf(cols * leaves, dtype=F32),
            buf(rows * leaves, dtype=F32),
            buf(3 * leaves, dtype=F32),
        ],
        compiler_params=params(),
    )(coupling_pairs, near_pairs, coupling_count, x_all, x_pts, w_all, coupling, near_blocks)
    out = pl.pallas_call(
        functools.partial(down_kernel, rows, cols),
        out_shape=jax.ShapeDtypeStruct((2 * q, piece), BF),
        in_specs=[VMEM] * 13,
        out_specs=VMEM,
        scratch_shapes=[
            buf(cols - 1, 2, packs),
            buf(deep, inner - 1, packs),
            buf(deep - 1, packs),
            buf(deep - 1, packs),
            buf(2, packs),
            buf(2 * (rows + cols), dtype=F32),
            sems(cols - 1),
            sems(deep, inner - 1),
            sems(deep - 1),
            sems(2),
        ],
        compiler_params=params(1),
    )(
        y_part, z_part, n_part, n0, n2, order2, ubasis, vbasis, leaf_up_u, leaf_up_v,
        transfer_u, transfer_v, upper_coupling,
    )
    return out[:q], out[q:]


def solution(mesh):
    both = P(None, ("row", "col"))
    flat = P(("row", "col"))
    return jax.shard_map(
        per_device,
        mesh=mesh,
        in_specs=(both, both, flat, both, both, both, both, both, both, flat, both, both, P(), P(), P()),
        out_specs=(both, both),
        check_vma=False,
    )
```
